32 devices in a mesh: seq: 4 (over y, x), wshard: 8 (over z, core).
Axes of the slice: x: 2, y: 2, z: 4, core: 2. Of those that a mesh axis runs over, the one named last changes fastest.
Arguments:
- inputs: bfloat16 [8, 1024, 1024], P('wshard', 'seq'), may hold values from -6 to 6
- routes: int32 [8, 1024, 1], P('wshard', 'seq'), may hold values from 0 to 3; in each aligned block of 256 rows (0 to 255, 256 to 511, ..., all dimensions but the last counted through in order) at most 96 rows name the same one
- block_ids: int32 [8, 1024], P('wshard'), may hold values from 0 to 7, never falling along the last dimension, each value on 1 to 256 neighbouring positions
- qkv_weight: bfloat16 [1024, 3072], P('wshard'), may hold values from -0.1875 to 0.1875
- out_weight: bfloat16 [1024, 1024], P('wshard'), may hold values from -3 to 3
- gain_one: bfloat16 [1024], P('wshard'), may hold values from 0.5 to 1.5
- gain_two: bfloat16 [1024], P('wshard'), may hold values from 0.5 to 1.5
- centroid: bfloat16 [4, 1024], replicated, may hold values from -0.125 to 0.125
- up_one: bfloat16 [8, 2048, 1024], P('wshard', 'seq'), may hold values from -0.1875 to 0.1875
- down_one: bfloat16 [8, 2048, 1024], P('wshard', 'seq'), may hold values from -0.09375 to 0.09375
- up_two: bfloat16 [8, 2048, 1024], P('wshard', 'seq'), may hold values from -0.1875 to 0.1875
- down_two: bfloat16 [8, 2048, 1024], P('wshard', 'seq'), may hold values from -0.09375 to 0.09375
- cotangent: bfloat16 [8, 1024, 1024], P('wshard', 'seq'), may hold values from -6 to 6
Outputs:
- layer_out: bfloat16 [8, 1024, 1024], P('wshard', 'seq')
- input_grad: bfloat16 [8, 1024, 1024], P('wshard', 'seq')
- qkv_grad: float32 [1024, 3072], P('wshard')
- out_grad: float32 [1024, 1024], P('wshard')
- gain_one_grad: float32 [1024], P('wshard')
- gain_two_grad: float32 [1024], P('wshard')
- centroid_grad: float32 [4, 1024], replicated
- up_one_grad: float32 [8, 2048, 1024], P('wshard', 'seq')
- down_one_grad: float32 [8, 2048, 1024], P('wshard', 'seq')
- up_two_grad: float32 [8, 2048, 1024], P('wshard', 'seq')
- down_two_grad: float32 [8, 2048, 1024], P('wshard', 'seq')
The draws below stay inside these ranges and needn't reach their ends.
Inputs may be any that keep to these rules, and one draw needn't show every extreme that they name: `routes`: among the 256 tokens of one device (aligned blocks of the flattened rows), no expert is named more than 96 times, and some device names one expert exactly 96 times. `block_ids`: along each sequence the block ids never fall, every id is used, each block spans 1 to 256 positions and one spans exactly 256.
All inputs are finite; a program needn't handle non-finite values.
Results may differ from the reference program's by a relative error of at most 0.015.
Values may be sent and summed in bfloat16 or wider, within the bound.
A program may use at most 256 MiB of HBM per device.

```python
import math
import jax
import jax.numpy as jnp
import numpy as np
from jax import lax

D = 1024
HEAD = 64
FF = 4096
BLOCK = 256
TOK_DEV = 256
SEQ_LEN = 1024
NSEQ = 8
EXP = 4
MOST = 96
LCAP = 72
CAP = 2304
N_SEQ = 4


def block_levels(stream_key, extent, shards, smallest, high):
    factor_of, own = 1.0, jax.random.fold_in(stream_key, 6)
    for position, shards_of in shards:
        heights = jnp.exp(jax.random.uniform(jax.random.fold_in(own, position), (shards_of,), jnp.float32, smallest / len(shards), high / len(shards)))
        factor_of = factor_of * jnp.repeat(heights, extent[position] // shards_of).reshape([-1 if axis == position else 1 for axis in range(len(extent))])
    return factor_of


def length_profile(count, total, reach, slope):
    portions = [(1 << 20) // math.isqrt(standing ** slope) + 1 for standing in range(2, count + 1)]
    surplus, given = total - reach - (count - 1), [1] * (count - 1)
    while surplus > 0:
        movable = [i for i in range(count - 1) if given[i] < reach]
        mass, budget = sum([portions[i] for i in movable]), surplus
        for i in movable:
            extra = min(reach - given[i], max(1, budget * portions[i] // mass), surplus)
            given[i] = given[i] + extra
            surplus = surplus - extra
    return np.array([reach] + given)


def ragged_sizes(stream_key, count, total, bound, lean):
    if count == 2:
        one = jax.random.randint(stream_key, (), max(1, total - bound), min(bound, total - 1) + 1)
        return jnp.stack([one, total - one])
    sizes = jnp.asarray(length_profile(count, total, bound, lean), jnp.int32)
    pairs = (count - 1) // 2
    source_of, receiver = sizes[1:1 + 2 * pairs:2], sizes[2:2 + 2 * pairs:2]
    room = jnp.minimum(source_of - 1, bound - receiver)
    moved = jax.random.randint(jax.random.fold_in(stream_key, 1), (pairs,), 0, 1 << 20) % (room + 1)
    sizes = sizes.at[1:1 + 2 * pairs:2].set(source_of - moved).at[2:2 + 2 * pairs:2].set(receiver + moved)
    return sizes[jax.random.permutation(jax.random.fold_in(stream_key, 2), count)]


def routed_block(rng, own, number, rows, amount, top, reach, lean):
    order = jax.random.permutation(rng, amount)
    heavy_load, common = shares(amount, rows * top, reach, lean, True), shares(amount, rows * top, reach, lean, False)
    places = jnp.arange(amount)

    def named(tallies, rotation):
        used = int((tallies > 0).sum())
        fixed = max(1, used // 4)
        moved = fixed + (places - fixed + rotation * (used - fixed)) % max(1, amount - fixed)
        return jnp.zeros((amount,), jnp.int32).at[order[jnp.where(places < fixed, places, moved)]].set(jnp.asarray(tallies, jnp.int32))

    tallies = jnp.where(number % 4 == 0, named(heavy_load, number // 4), named(common, number - number // 4 - 1))
    mixed = jax.random.permutation(jax.random.fold_in(own, 3), amount)
    source_of, taker = mixed[0:amount // 2 * 2:2], mixed[1:amount // 2 * 2:2]
    margin = jnp.minimum(tallies[source_of] - 1, reach - tallies[taker]) // 2
    margin = jnp.where((source_of == order[0]) | (taker == order[0]) | (tallies[taker] == 0), 0, jnp.maximum(margin, 0))
    moved = jax.random.randint(jax.random.fold_in(own, 4), (amount // 2,), 0, 1 << 20) % (margin + 1)
    tallies = tallies.at[source_of].add(-moved).at[taker].add(moved)
    labels = jnp.searchsorted(jnp.cumsum(tallies), jnp.arange(rows * top), side="right").astype(jnp.int32)
    listing = labels.reshape(top, rows).T
    listing = listing[jax.random.permutation(jax.random.fold_in(own, 1), rows)]
    rotation = jax.random.randint(jax.random.fold_in(own, 2), (rows, 1), 0, top)
    return jnp.take_along_axis(listing, (jnp.arange(top)[None, :] + rotation) % top, axis=1)


def shares(number_of, total, most, lean, full):
    loads = [(1 << 20) // math.isqrt(standing ** lean) + 1 for standing in range(1, number_of + 1)]
    largest = most if full else min(most, max(-(-total // number_of), total * loads[0] // sum(loads)))
    least = 1 if total - largest >= number_of - 1 else 0
    holding, rest = [largest] + [least] * (number_of - 1), total - largest - least * (number_of - 1)
    while rest > 0:
        free = [i for i in range(1, number_of) if holding[i] < largest] or [i for i in range(1, number_of) if holding[i] < most]
        mass, budget = sum([loads[i] for i in free]), rest
        for i in free:
            extra = min(most - holding[i], max(1, budget * loads[i] // mass), rest)
            holding[i] = holding[i] + extra
            rest = rest - extra
    return np.array(holding)


def centred(key, dims, width, bound, split=(), kind=jnp.bfloat16):
    result = jax.random.normal(key, dims, jnp.float32) * width
    if len(split) > 0:
        result = block_levels(key, dims, split, -0.22, 0.18) * result
    return jnp.clip(result, min=-bound, max=bound).astype(kind)


def setup_inputs(seed: int = 0) -> dict:
    splits = jax.random.split(jax.random.key(seed), 14)
    inputs = centred(splits[0], (NSEQ, SEQ_LEN, D), 1.0, 6.0, ((0, 8), (1, 4)))
    routes_keys = jax.random.split(jax.random.fold_in(splits[1], 1), NSEQ * SEQ_LEN // TOK_DEV)
    routes_turns = jax.random.permutation(jax.random.fold_in(splits[1], 3), NSEQ * SEQ_LEN // TOK_DEV)
    routes = jax.vmap(lambda own, number: routed_block(jax.random.fold_in(splits[1], 2), own, number, TOK_DEV, EXP, 1, MOST, 4))(routes_keys, routes_turns).reshape((NSEQ, SEQ_LEN, 1))
    block_ids = jax.vmap(lambda own: jnp.searchsorted(jnp.cumsum(ragged_sizes(own, 2 * SEQ_LEN // BLOCK, SEQ_LEN, BLOCK, 1)), jnp.arange(SEQ_LEN), side="right"))(jax.random.split(splits[2], NSEQ)).reshape((NSEQ, SEQ_LEN)).astype(jnp.int32)
    qkv_weight = centred(splits[3], (D, 3 * D), D ** -0.5, 0.1875, ((0, 8),))
    out_weight = centred(splits[4], (D, D), (max(1, D // 256)) ** -0.5, 3.0, ((0, 8),))
    gain_one = jnp.clip(1.0 + 0.1 * jax.random.normal(splits[5], (D,), jnp.float32), 0.5, 1.5).astype(jnp.bfloat16)
    gain_two = jnp.clip(1.0 + 0.1 * jax.random.normal(splits[6], (D,), jnp.float32), 0.5, 1.5).astype(jnp.bfloat16)
    centroid = centred(splits[7], (EXP, D), (2 * D) ** -0.5, 0.125)
    up_one = centred(splits[8], (2 * EXP, FF // 2, D), D ** -0.5, 0.1875, ((0, 8), (1, 4)))
    down_one = centred(splits[9], (2 * EXP, FF // 2, D), FF ** -0.5, 0.09375, ((0, 8), (1, 4)))
    up_two = centred(splits[10], (2 * EXP, FF // 2, D), D ** -0.5, 0.1875, ((0, 8), (1, 4)))
    down_two = centred(splits[11], (2 * EXP, FF // 2, D), FF ** -0.5, 0.09375, ((0, 8), (1, 4)))
    cotangent = centred(splits[12], (NSEQ, SEQ_LEN, D), 1.0, 6.0, ((0, 8), (1, 4)))
    return {"inputs": inputs, "routes": routes, "block_ids": block_ids, "qkv_weight": qkv_weight, "out_weight": out_weight, "gain_one": gain_one, "gain_two": gain_two, "centroid": centroid, "up_one": up_one, "down_one": down_one, "up_two": up_two, "down_two": down_two, "cotangent": cotangent}


@jax.custom_vjp
def low(v):
    return lax.optimization_barrier(v.astype(jnp.bfloat16)).astype(jnp.float32)

@jax.custom_vjp
def low_back(v):
    return v

def low_keep(v):
    return (low(v), None)

def low_pass(kept, grad):
    return (grad,)

def back_keep(v):
    return (v, None)

def back_low(kept, grad):
    return (low(grad),)
low.defvjp(low_keep, low_pass)
low_back.defvjp(back_keep, back_low)
EPSILON = 1e-05
NEG_FILL = -1e+30
HIGH = lax.Precision.HIGHEST

def norm_rows(values, gain_vec):
    centre = lax.optimization_barrier(jnp.mean(values, axis=-1, keepdims=True))
    shifted = values - centre
    spread = lax.optimization_barrier(jnp.mean(shifted * shifted, axis=-1, keepdims=True))
    return shifted * lax.rsqrt(spread + EPSILON) * gain_vec

def attend_group(attn_params, group_in, group_blocks):
    qkv_mat, out_mat, gain_vec = attn_params
    count_g, length, model_width = group_in.shape
    heads_n = model_width // HEAD
    normed = low(norm_rows(group_in, gain_vec))
    projected = low_back(low(jnp.einsum('gld,de->gle', normed, qkv_mat, precision=HIGH)))
    queries = projected[..., :model_width].reshape(count_g, length, heads_n, HEAD)
    keys_all = projected[..., model_width:2 * model_width].reshape(count_g, length, heads_n, HEAD)
    values_all = projected[..., 2 * model_width:].reshape(count_g, length, heads_n, HEAD)
    scores = low_back(jnp.einsum('gqhc,gkhc->ghqk', queries, keys_all, precision=HIGH) * HEAD ** (-0.5))
    allowed = group_blocks[:, None, None, :] <= group_blocks[:, None, :, None]
    scores = jnp.where(allowed, scores, NEG_FILL)
    prob_low = low(jax.nn.softmax(scores, axis=-1))
    mixed_heads = jnp.einsum('ghqk,gkhc->gqhc', prob_low, values_all, precision=HIGH)
    mixed_heads = low_back(low(mixed_heads.reshape(count_g, length, model_width)))
    branch = low_back(jnp.einsum('gld,de->gle', mixed_heads, out_mat, precision=HIGH))
    return group_in + branch

def expert_run(packed):
    up_a, down_a, up_b, down_b, block_in = packed
    pre_one = low_back(jnp.dot(block_in, up_a.T, precision=HIGH))
    act_one = low(jax.nn.gelu(pre_one, approximate=False))
    first_out = low_back(low(block_in + jnp.dot(act_one, down_a, precision=HIGH)))
    pre_two = low_back(jnp.dot(first_out, up_b.T, precision=HIGH))
    act_two = low(jax.nn.gelu(pre_two, approximate=False))
    return low_back(low(first_out + jnp.dot(act_two, down_b, precision=HIGH)))

def forward(params, inputs_f, route_flat, block_ids, kept_f, slot_flat):
    qkv_mat, out_mat, gain_a, gain_b, centroid_f, up_a, down_a, up_b, down_b = params
    group_size = math.gcd(NSEQ, max(1, 4096 // SEQ_LEN))
    stepper = jax.checkpoint(attend_group)

    def run_group(group_item):
        return stepper((qkv_mat, out_mat, gain_a), group_item[0], group_item[1])
    grouped_out = lax.map(run_group, (inputs_f.reshape(NSEQ // group_size, group_size, SEQ_LEN, D), block_ids.reshape(NSEQ // group_size, group_size, SEQ_LEN)))
    hidden = grouped_out.reshape(NSEQ * SEQ_LEN, D)
    normed_two = low(norm_rows(hidden, gain_b))
    sent_rows = low_back(normed_two)
    logits = jnp.dot(normed_two, centroid_f.T, precision=HIGH)
    expert_hot = (route_flat[:, None] == jnp.arange(EXP, dtype=jnp.int32)[None, :]).astype(hidden.dtype)
    chosen = lax.optimization_barrier(jnp.sum(logits * expert_hot, axis=1))
    gate_val = jax.nn.sigmoid(chosen) * kept_f
    blocks_in = jnp.zeros((EXP, CAP, D), hidden.dtype).at[route_flat, slot_flat].add(sent_rows * kept_f[:, None])
    experts_out = lax.map(jax.checkpoint(expert_run), (up_a.reshape(EXP, FF, D), down_a.reshape(EXP, FF, D), up_b.reshape(EXP, FF, D), down_b.reshape(EXP, FF, D), blocks_in))
    returned = experts_out[route_flat, slot_flat] * kept_f[:, None]
    return (hidden + gate_val[:, None] * returned).reshape(NSEQ, SEQ_LEN, D)

def reference(inputs, routes, block_ids, qkv_weight, out_weight, gain_one, gain_two, centroid, up_one, down_one, up_two, down_two, cotangent):
    route_ids = routes[..., 0].astype(jnp.int32)
    group_view = route_ids.reshape(NSEQ * N_SEQ, TOK_DEV)
    route_hot = (group_view[:, :, None] == jnp.arange(EXP, dtype=jnp.int32)[None, None, :]).astype(jnp.int32)
    slot_rank = lax.optimization_barrier(jnp.sum((jnp.cumsum(route_hot, axis=1) - 1) * route_hot, axis=2))
    kept_f = (slot_rank < LCAP).astype(jnp.float32).reshape(-1)
    group_index = jnp.arange(NSEQ * N_SEQ, dtype=jnp.int32)[:, None]
    slot_flat = (group_index * LCAP + jnp.minimum(slot_rank, LCAP - 1)).astype(jnp.int32).reshape(-1)
    route_flat = route_ids.reshape(-1)
    params = (qkv_weight.astype(jnp.float32), out_weight.astype(jnp.float32), gain_one.astype(jnp.float32), gain_two.astype(jnp.float32), centroid.astype(jnp.float32), up_one.astype(jnp.float32), down_one.astype(jnp.float32), up_two.astype(jnp.float32), down_two.astype(jnp.float32))

    def layer_fn(param_set, input_set):
        return forward(param_set, input_set, route_flat, block_ids, kept_f, slot_flat)
    layer_out, pullback = jax.vjp(layer_fn, params, inputs.astype(jnp.float32))
    param_grads, input_grad = pullback(cotangent.astype(jnp.float32))
    return (layer_out.astype(jnp.bfloat16), input_grad.astype(jnp.bfloat16), param_grads[0], param_grads[1], param_grads[2], param_grads[3], param_grads[4], param_grads[5], param_grads[6], param_grads[7], param_grads[8])
```

```python
import jax
import jax.numpy as jnp
from jax import lax
from jax.sharding import PartitionSpec as P

HEAD = 64


EPSILON = 1e-05
NEG_FILL = -1e30


def as_sent(shard):

    def short(part):
        return part.astype(jnp.bfloat16) if part.dtype == jnp.float32 else part

    return jax.tree.map(short, shard)


def from_partner(shard, axis, distance):
    return lax.ppermute(shard, axis, [(i, i ^ 1 << distance) for i in range(lax.axis_size(axis))])


def norm_rows(values, gain_vec):
    centre = jnp.mean(values, axis=-1, keepdims=True)
    shifted = values - centre
    spread = jnp.mean(shifted * shifted, axis=-1, keepdims=True)
    return shifted * lax.rsqrt(spread + EPSILON) * gain_vec


def gelu_exact(argument):
    return jax.nn.gelu(argument, approximate=False)


def gelu_back(pre_act, upstream):
    return jax.vjp(gelu_exact, pre_act)[1](upstream)[0]


def dot_rows(left_mat, right_mat):
    return lax.dot_general(
        left_mat, right_mat, (((0,), (0,)), ((), ())), preferred_element_type=jnp.float32
    )


def dot_last(left_mat, right_mat):
    return lax.dot_general(
        left_mat, right_mat, (((1,), (1,)), ((), ())), preferred_element_type=jnp.float32
    )


def heads_layout(parts_tuple):
    return jax.tree.map(
        lambda part, own: part.astype(own.dtype),
        lax.all_to_all(as_sent(parts_tuple), "seq", split_axis=1, concat_axis=0, tiled=True),
        parts_tuple,
    )


def tokens_layout(parts_tuple):
    return jax.tree.map(
        lambda part, own: part.astype(own.dtype),
        lax.all_to_all(as_sent(parts_tuple), "seq", split_axis=0, concat_axis=1, tiled=True),
        parts_tuple,
    )


def attend_forward(query_head, key_head, value_head, block_row, score_scale):
    length = query_head.shape[0]
    block_span = min(512, length)
    heads_here = query_head.shape[1] // HEAD
    keys_split = key_head.reshape(length, heads_here, HEAD)
    values_split = value_head.reshape(length, heads_here, HEAD)

    def one_block(start_row):
        query_part = lax.dynamic_slice_in_dim(query_head, start_row, block_span, 0).reshape(
            block_span, heads_here, HEAD
        )
        block_part = lax.dynamic_slice_in_dim(block_row, start_row, block_span, 0)
        scores = (
            jnp.einsum("qhc,khc->hqk", query_part, keys_split, preferred_element_type=jnp.float32)
            * score_scale
        )
        allowed = block_row[None, None, :] <= block_part[None, :, None]
        scores = jnp.where(allowed, scores, NEG_FILL)
        row_top = jnp.max(scores, axis=2, keepdims=True)
        weights = jnp.exp(scores - row_top)
        row_total = jnp.sum(weights, axis=2, keepdims=True)
        prob_low = (weights / row_total).astype(jnp.bfloat16)
        mixed_out = jnp.einsum(
            "hqk,khc->qhc", prob_low, values_split, preferred_element_type=jnp.float32
        )
        return (
            mixed_out.reshape(block_span, heads_here * HEAD).astype(jnp.bfloat16),
            (row_top + jnp.log(row_total))[:, :, 0],
        )

    starts = jnp.arange(length // block_span, dtype=jnp.int32) * block_span
    mixed_blocks, lse_blocks = lax.map(one_block, starts)
    return (
        mixed_blocks.reshape(length, heads_here * HEAD),
        jnp.transpose(lse_blocks, (1, 0, 2)).reshape(heads_here, length),
    )


def attend_backward(query_head, key_head, value_head, block_row, log_total, grad_head, score_scale):
    length = query_head.shape[0]
    block_span = min(512, length)
    heads_here = query_head.shape[1] // HEAD
    keys_split = key_head.reshape(length, heads_here, HEAD)
    values_split = value_head.reshape(length, heads_here, HEAD)

    def one_block(carry, start_row):
        key_acc, value_acc = carry
        query_part = lax.dynamic_slice_in_dim(query_head, start_row, block_span, 0).reshape(
            block_span, heads_here, HEAD
        )
        grad_part = lax.dynamic_slice_in_dim(grad_head, start_row, block_span, 0).reshape(
            block_span, heads_here, HEAD
        )
        block_part = lax.dynamic_slice_in_dim(block_row, start_row, block_span, 0)
        lse_part = lax.dynamic_slice_in_dim(log_total, start_row, block_span, 1)
        scores = (
            jnp.einsum("qhc,khc->hqk", query_part, keys_split, preferred_element_type=jnp.float32)
            * score_scale
        )
        allowed = block_row[None, None, :] <= block_part[None, :, None]
        scores = jnp.where(allowed, scores, NEG_FILL)
        prob_full = jnp.exp(scores - lse_part[:, :, None])
        prob_low = prob_full.astype(jnp.bfloat16)
        d_prob = jnp.einsum(
            "qhc,khc->hqk", grad_part, values_split, preferred_element_type=jnp.float32
        )
        row_dot = jnp.sum(prob_full * d_prob, axis=2, keepdims=True)
        d_scores = (prob_full * (d_prob - row_dot)).astype(jnp.bfloat16)
        d_query = (
            jnp.einsum("hqk,khc->qhc", d_scores, keys_split, preferred_element_type=jnp.float32)
            * score_scale
        )
        key_acc = (
            key_acc
            + jnp.einsum("hqk,qhc->khc", d_scores, query_part, preferred_element_type=jnp.float32)
            * score_scale
        )
        value_acc = value_acc + jnp.einsum(
            "hqk,qhc->khc", prob_low, grad_part, preferred_element_type=jnp.float32
        )
        return (
            (key_acc, value_acc),
            d_query.reshape(block_span, heads_here * HEAD).astype(jnp.bfloat16),
        )

    starts = jnp.arange(length // block_span, dtype=jnp.int32) * block_span
    zeros_acc = jnp.zeros((length, heads_here, HEAD), jnp.float32)
    (key_acc, value_acc), query_blocks = lax.scan(one_block, (zeros_acc, zeros_acc), starts)
    flat_width = heads_here * HEAD
    return (
        query_blocks.reshape(length, flat_width),
        key_acc.reshape(length, flat_width).astype(jnp.bfloat16),
        value_acc.reshape(length, flat_width).astype(jnp.bfloat16),
    )


def local(
    inputs,
    routes,
    block_ids,
    qkv_weight,
    out_weight,
    gain_one,
    gain_two,
    centroid,
    up_one,
    down_one,
    up_two,
    down_two,
    cotangent,
):
    tok_count = inputs.shape[1]
    model_width = inputs.shape[2]
    exp_count = centroid.shape[0]
    seq_size = lax.axis_size("seq")
    wshard_size = lax.axis_size("wshard")
    slots = max(1, 9 * tok_count // (8 * exp_count))
    score_scale = HEAD ** (-0.5)
    head_width = model_width // seq_size
    seq_index = lax.axis_index("seq")
    same_core = [list(range(core, wshard_size, 2)) for core in range(2)]

    qkv_parts = qkv_weight.reshape(-1, 3, model_width)
    qkv_own = lax.dynamic_slice_in_dim(qkv_parts, seq_index * head_width, head_width, 2)
    qkv_heads = lax.all_gather(
        qkv_own.reshape(-1, 3 * head_width), "wshard", axis=0, tiled=True
    )
    full_gain_one = lax.all_gather(gain_one, "wshard", axis=0, tiled=True)
    full_gain_two = lax.all_gather(gain_two, "wshard", axis=0, tiled=True)
    gain_first = full_gain_one.astype(jnp.float32)
    gain_second = full_gain_two.astype(jnp.float32)
    tokens_in = inputs[0].astype(jnp.float32)
    normed_one = norm_rows(tokens_in, gain_first).astype(jnp.bfloat16)
    normed_all = lax.all_gather(normed_one, "seq", axis=0, tiled=True)
    full_out = lax.all_gather(out_weight, "wshard", axis=0, tiled=True)
    up_a, down_a, up_b, down_b = (
        lax.all_gather(part[0], "seq", axis=0, tiled=True)
        for part in (up_one, down_one, up_two, down_two)
    )
    projected = jnp.dot(normed_all, qkv_heads, preferred_element_type=jnp.float32).astype(
        jnp.bfloat16
    )
    query_head = projected[:, :head_width]
    key_head = projected[:, head_width : 2 * head_width]
    value_head = projected[:, 2 * head_width :]
    block_row = block_ids[0]
    mixed_head, log_total = attend_forward(query_head, key_head, value_head, block_row, score_scale)
    (mixed_tok,) = tokens_layout((mixed_head,))
    hidden = tokens_in + jnp.dot(mixed_tok, full_out, preferred_element_type=jnp.float32)
    normed_two = norm_rows(hidden, gain_second).astype(jnp.bfloat16)
    route_ids = routes[0, :, 0]
    expert_ids = jnp.arange(exp_count, dtype=jnp.int32)
    expert_hot = route_ids[:, None] == expert_ids[None, :]
    hot_low = expert_hot.astype(jnp.bfloat16)
    logits = dot_last(normed_two, centroid)
    chosen = jnp.sum(jnp.where(expert_hot, logits, 0.0), axis=1)
    sigmoid_val = jax.nn.sigmoid(chosen)
    positions = jnp.arange(tok_count, dtype=jnp.int32)
    lower_tri = (positions[:, None] >= positions[None, :]).astype(jnp.bfloat16)
    running = jnp.dot(lower_tri, hot_low, preferred_element_type=jnp.float32)
    local_rank = (jnp.sum(jnp.where(expert_hot, running, 0.0), axis=1) - 1.0).astype(jnp.int32)
    kept_mask = local_rank < slots
    gate_val = jnp.where(kept_mask, sigmoid_val, 0.0)
    slot_id = route_ids * slots + local_rank
    slot_ids = jnp.arange(exp_count * slots, dtype=jnp.int32)
    dispatch = ((slot_ids[:, None] == slot_id[None, :]) & kept_mask[None, :]).astype(jnp.bfloat16)
    dy_rows = cotangent[0].astype(jnp.float32)

    def exchange(slab):
        return lax.all_to_all(
            slab, "wshard", split_axis=0, concat_axis=0, axis_index_groups=same_core, tiled=True
        )

    both = jnp.concatenate((normed_two, (gate_val[:, None] * dy_rows).astype(jnp.bfloat16)), axis=1)
    packed = jnp.dot(dispatch, both, preferred_element_type=jnp.float32).astype(jnp.bfloat16)
    own_both = exchange(packed.reshape(exp_count, slots, 2 * model_width)).reshape(
        exp_count * slots, 2 * model_width
    )
    pair_both = from_partner(own_both, "wshard", 0)
    sent_all = jnp.concatenate((own_both[:, :model_width], pair_both[:, :model_width]), axis=0)
    d_second_all = jnp.concatenate((own_both[:, model_width:], pair_both[:, model_width:]), axis=0)
    own_rows = exp_count * slots

    def pair_total(partial_sum):
        other = from_partner(partial_sum, "wshard", 0)
        return partial_sum + jnp.concatenate((other[own_rows:], other[:own_rows]), axis=0)

    def add_rows(base, term):
        return (base.astype(jnp.float32) + term).astype(jnp.bfloat16)

    pre_one = dot_last(sent_all, up_a)
    act_one = gelu_exact(pre_one).astype(jnp.bfloat16)
    first_all = add_rows(
        sent_all, pair_total(jnp.dot(act_one, down_a, preferred_element_type=jnp.float32))
    )
    pre_two = dot_last(first_all, up_b)
    act_two = gelu_exact(pre_two).astype(jnp.bfloat16)
    second_part = jnp.dot(act_two, down_b, preferred_element_type=jnp.float32)
    second_own = add_rows(
        first_all[:own_rows],
        second_part[:own_rows] + from_partner(second_part[own_rows:], "wshard", 0),
    )
    d_pre_two = gelu_back(pre_two, dot_last(d_second_all, down_b)).astype(jnp.bfloat16)
    d_first_all = add_rows(
        d_second_all, pair_total(jnp.dot(d_pre_two, up_b, preferred_element_type=jnp.float32))
    )
    d_pre_one = gelu_back(pre_one, dot_last(d_first_all, down_a)).astype(jnp.bfloat16)
    d_sent_part = jnp.dot(d_pre_one, up_a, preferred_element_type=jnp.float32)
    d_sent_own = add_rows(
        d_first_all[:own_rows],
        d_sent_part[:own_rows] + from_partner(d_sent_part[own_rows:], "wshard", 0),
    )

    def weight_grad(left, right):
        return lax.psum_scatter(
            dot_rows(left, right).astype(jnp.bfloat16), "seq", scatter_dimension=0, tiled=True
        ).astype(jnp.float32)

    grad_down_b = weight_grad(act_two, d_second_all)
    grad_up_b = weight_grad(d_pre_two, first_all)
    grad_down_a = weight_grad(act_one, d_first_all)
    grad_up_a = weight_grad(d_pre_one, sent_all)

    def give_back(rows):
        return dot_rows(
            dispatch,
            exchange(rows.reshape(exp_count, slots, model_width)).reshape(own_rows, model_width),
        )

    returned_tok = give_back(second_own)
    layer_out = (hidden + gate_val[:, None] * returned_tok).astype(jnp.bfloat16)
    d_gate = jnp.where(kept_mask, jnp.sum(dy_rows * returned_tok, axis=1), 0.0)
    d_chosen = d_gate * sigmoid_val * (1.0 - sigmoid_val)
    d_sent_tok = give_back(d_sent_own)
    centroid_tok = jnp.dot(hot_low, centroid, preferred_element_type=jnp.float32)
    d_normed_two = d_sent_tok + d_chosen[:, None] * centroid_tok
    centroid_term = lax.dot_general(
        expert_hot.astype(jnp.float32),
        d_chosen[:, None] * normed_two.astype(jnp.float32),
        (((0,), (0,)), ((), ())),
        precision=lax.Precision.HIGHEST,
        preferred_element_type=jnp.float32,
    )
    norm_two_back = jax.vjp(norm_rows, hidden, gain_second)[1]
    d_hidden_norm, d_gain_second = norm_two_back(d_normed_two)
    d_hidden = dy_rows + d_hidden_norm
    d_branch = d_hidden.astype(jnp.bfloat16)
    grad_out_full = dot_rows(mixed_tok, d_branch)
    d_mixed = dot_last(d_branch, full_out).astype(jnp.bfloat16)
    (d_mixed_head,) = heads_layout((d_mixed,))
    d_query, d_key, d_value = attend_backward(
        query_head, key_head, value_head, block_row, log_total, d_mixed_head, score_scale
    )
    d_projected = jnp.concatenate((d_query, d_key, d_value), axis=1)
    grad_qkv_heads = dot_rows(normed_all, d_projected)
    d_normed_part = dot_last(d_projected, qkv_heads)
    d_normed_one = lax.psum_scatter(
        d_normed_part.astype(jnp.bfloat16), "seq", scatter_dimension=0, tiled=True
    ).astype(jnp.float32)
    norm_one_back = jax.vjp(norm_rows, tokens_in, gain_first)[1]
    d_tokens_norm, d_gain_first = norm_one_back(d_normed_one)
    input_grad = (d_hidden + d_tokens_norm).astype(jnp.bfloat16)
    qkv_sum = lax.psum_scatter(grad_qkv_heads, "wshard", scatter_dimension=0, tiled=True)
    qkv_all = lax.all_gather(qkv_sum.astype(jnp.bfloat16), "seq", axis=0, tiled=False)
    qkv_rows = qkv_sum.shape[0]
    grad_qkv = (
        jnp.transpose(qkv_all.reshape(seq_size, qkv_rows, 3, head_width), (1, 2, 0, 3))
        .reshape(qkv_rows, 3 * model_width)
        .astype(jnp.float32)
    )
    out_part = lax.psum_scatter(grad_out_full, "wshard", scatter_dimension=0, tiled=True)
    grad_out = lax.psum(out_part.astype(jnp.bfloat16), "seq").astype(jnp.float32)
    small = jnp.concatenate((d_gain_first[None], d_gain_second[None], centroid_term), axis=0)
    small = lax.psum(small, ("seq", "wshard"))
    gain_rows = gain_one.shape[0]
    gain_at = lax.axis_index("wshard") * gain_rows
    grad_gain_one = lax.dynamic_slice_in_dim(small[0], gain_at, gain_rows, 0)
    grad_gain_two = lax.dynamic_slice_in_dim(small[1], gain_at, gain_rows, 0)
    grad_centroid = small[2:]
    return (
        layer_out[None],
        input_grad[None],
        grad_qkv,
        grad_out,
        grad_gain_one,
        grad_gain_two,
        grad_centroid,
        grad_up_a[None],
        grad_down_a[None],
        grad_up_b[None],
        grad_down_b[None],
    )


def solution(mesh):
    return jax.shard_map(
        local,
        mesh=mesh,
        in_specs=(
            P("wshard", "seq", None),
            P("wshard", "seq", None),
            P("wshard", None),
            P("wshard", None),
            P("wshard", None),
            P("wshard"),
            P("wshard"),
            P(),
            P("wshard", "seq", None),
            P("wshard", "seq", None),
            P("wshard", "seq", None),
            P("wshard", "seq", None),
            P("wshard", "seq", None),
        ),
        out_specs=(
            P("wshard", "seq", None),
            P("wshard", "seq", None),
            P("wshard", None),
            P("wshard", None),
            P("wshard"),
            P("wshard"),
            P(),
            P("wshard", "seq", None),
            P("wshard", "seq", None),
            P("wshard", "seq", None),
            P("wshard", "seq", None),
        ),
        check_vma=False,
    )
```
